32 devices in a mesh: tile: 4 (over y, x), atom: 8 (over z, core).
Axes of the slice: x: 2, y: 2, z: 4, core: 2. Of those that a mesh axis runs over, the one named last changes fastest.
Arguments:
- image: bfloat16 [64, 32, 512], P(None, 'tile'), may hold values from -10 to 10
- coeffs: bfloat16 [512, 32, 512], P('atom', 'tile'), may hold values from -5 to 5
- dictionary: bfloat16 [512, 5184], P('atom'), may hold values from -0.078125 to 0.078125
- shrink: float32 [512], P('atom'), may hold values from 0.05 to 0.5
- seam_map: int32 [4, 512], replicated, may hold values from 0 to 1
Outputs:
- new_coeffs: bfloat16 [512, 32, 512], P('atom', 'tile')
- residual: bfloat16 [64, 32, 512], P(None, 'tile')
- atom_step: float32 [512, 5184], P('atom', 'tile')
The draws below stay inside these ranges and needn't reach their ends.
All inputs are finite; a program needn't handle non-finite values.
Results may differ from the reference program's by a relative error of at most 0.0029.
Values may be sent and summed in bfloat16 or wider, within the bound.
A program may use at most 64 MiB of HBM per device.

```python
import math
import jax
import jax.numpy as jnp
from jax import lax

C = 64
K = 512
TAP = 9
TILE_W = 512
STRIPS = 4
H = 32


def plant(entries, rng, least, largest):
    extent = entries.shape
    index_at = [jax.random.randint(jax.random.fold_in(rng, axis), (), 0, extent[axis]) for axis in range(len(extent))]
    entries = entries.at[tuple(index_at)].set(least)
    longest = extent.index(max(extent))
    index_at[longest] = (index_at[longest] + 1) % extent[longest]
    return entries.at[tuple(index_at)].set(largest)


def shard_levels(key, dims, pieces, smallest, top_value):
    level = 1.0
    for axis_at, blocks in pieces:
        heights = jax.random.uniform(jax.random.fold_in(jax.random.fold_in(key, 6), axis_at), (blocks,), jnp.float32, smallest / len(pieces), top_value / len(pieces))
        level = level * jnp.repeat(jnp.exp(heights), dims[axis_at] // blocks).reshape((-1,) + (1,) * (len(dims) - 1 - axis_at))
    return level


def gaussian(own_key, dims, spread, bound, cuts=(), kind=jnp.bfloat16):
    drawn = spread * jax.random.normal(own_key, dims, jnp.float32)
    if cuts:
        drawn = drawn * shard_levels(own_key, dims, cuts, -0.22, 0.18)
    return jnp.clip(drawn, -bound, bound).astype(kind)


def setup_inputs(seed: int = 0) -> dict:
    streams_of = jax.random.split(jax.random.key(seed), 6)
    return {
        "image": gaussian(streams_of[0], (C, H, TILE_W), 2.0, 10.0, ((1, 4),)),
        "coeffs": gaussian(streams_of[1], (K, H, TILE_W), 1.0, 5.0, ((0, 8), (1, 4))),
        "dictionary": gaussian(streams_of[2], (K, C * TAP * TAP), (C * TAP * TAP) ** -0.5, 0.078125, ((0, 8),)),
        "shrink": jnp.clip(jnp.exp(math.log(0.5) - 2.3025851 * jax.random.uniform(streams_of[3], (K,), jnp.float32) ** shard_levels(streams_of[3], (K,), ((0, 8),), -0.2, 0.2)), 0.05, 0.5),
        "seam_map": plant(jax.random.randint(streams_of[4], (STRIPS, TILE_W), 0, 2), jax.random.fold_in(streams_of[4], 1), 0, 1).astype(jnp.int32),
    }


step_size = 0.1
eps_sq = 0.01

def pad_strips(field, seam_map):
    chans, rows, cols = field.shape
    strips = seam_map.shape[0]
    strip_rows = rows // strips
    tiled = field.reshape(chans, strips, strip_rows, cols).transpose(1, 0, 2, 3)
    w_down = (0.5 + 0.5 * seam_map.astype(jnp.float32)).astype(field.dtype)
    w_up = jnp.roll(w_down, 1, axis=0)
    upper = jnp.roll(tiled, 1, axis=0)[:, :, strip_rows - 4:] * w_up[:, None, None, :]
    lower = jnp.roll(tiled, -1, axis=0)[:, :, :4] * w_down[:, None, None, :]
    joined = jnp.concatenate([upper, tiled, lower], axis=2)
    return jnp.pad(joined, ((0, 0), (0, 0), (0, 0), (4, 4)))

def correlate(lhs, rhs):
    return lax.conv_general_dilated(lhs.astype(jnp.float32), rhs.astype(jnp.float32), (1, 1), 'VALID', dimension_numbers=('NCHW', 'OIHW', 'NCHW'), precision=lax.Precision.HIGHEST)

def reference(image, coeffs, dictionary, shrink, seam_map):
    strips = seam_map.shape[0]
    strip_rows = image.shape[1] // strips
    kernel = dictionary.reshape(K, C, TAP, TAP)
    coef_padded = pad_strips(coeffs, seam_map)
    synth_kernel = kernel.transpose(1, 0, 2, 3)

    def synth_one(block):
        return correlate(block[None], synth_kernel)[0]
    synthesis = lax.map(synth_one, coef_padded)
    image_tiles = image.reshape(C, strips, strip_rows, TILE_W).transpose(1, 0, 2, 3)
    resid_tiles = (image_tiles.astype(jnp.float32) - synthesis).astype(jnp.bfloat16)
    residual = resid_tiles.transpose(1, 0, 2, 3).reshape(C, H, TILE_W)
    resid_padded = pad_strips(residual, seam_map)
    coef_tiles = coeffs.reshape(K, strips, strip_rows, TILE_W).transpose(1, 0, 2, 3)
    flipped = kernel[:, :, ::-1, ::-1]

    def strip_terms(pair):
        padded, own = pair
        corr = correlate(padded[None], flipped)[0]
        terms = correlate(padded[:, None], own[:, None])
        return (corr, terms)
    corr_tiles, term_tiles = lax.map(strip_terms, (resid_padded, coef_tiles))
    correlation = corr_tiles.transpose(1, 0, 2, 3).reshape(K, H, TILE_W)
    updated = coeffs.astype(jnp.float32) + step_size * correlation
    new_coeffs = (updated - shrink[:, None, None] * updated / jnp.sqrt(updated * updated + eps_sq)).astype(jnp.bfloat16)
    summed = lax.optimization_barrier(jnp.sum(term_tiles, axis=0))
    scale = 1.0 / jnp.sqrt(jnp.float32(H * TILE_W))
    atom_step = summed[:, :, ::-1, ::-1].transpose(1, 0, 2, 3).reshape(K, C * TAP * TAP) * scale
    return (new_coeffs, residual, atom_step)
```

```python
import jax
import jax.numpy as jnp
from jax import lax
from jax.sharding import PartitionSpec as P

TAP = 9
RIM = TAP // 2
BLOCK = 4
SPAN = BLOCK + TAP - 1

step_size = 0.1
eps_sq = 0.01


def rims(block):
    count = lax.axis_size("tile")
    forward = [(i, (i + 1) % count) for i in range(count)]
    backward = [(target, source) for source, target in forward]
    low = lax.ppermute(block[-RIM:], "tile", forward)
    high = lax.ppermute(block[:RIM], "tile", backward)
    return low, high


def columns(padded, width):
    wide = jnp.pad(padded, ((0, 0), (0, 0), (RIM, RIM)))
    return jnp.stack([wide[:, :, d : d + width] for d in range(TAP)], axis=1)


def banded(taps):
    parts = [
        jnp.pad(taps, ((j, BLOCK - 1 - j), (0, 0), (0, 0), (0, 0))) for j in range(BLOCK)
    ]
    return jnp.concatenate(parts, axis=3).reshape(SPAN * TAP * taps.shape[2], -1)


def windows(cols, rows):
    for start in range(0, rows, BLOCK):
        part = cols[start : start + SPAN]
        yield start, part.reshape(-1, part.shape[-1])


def apply_band(cols, band, rows):
    outs = []
    for _, window in windows(cols, rows):
        outs.append(
            lax.dot_general(
                band, window, (((0,), (0,)), ((), ())), preferred_element_type=jnp.float32
            )
        )
    return jnp.concatenate(outs, axis=0).reshape(rows, -1, cols.shape[-1])


def per_device(image, coeffs, dictionary, shrink, seam_map):
    local_atoms, strip_rows, width = coeffs.shape
    chans = image.shape[0]
    strips = lax.axis_size("tile")
    position = lax.axis_index("tile")
    seam_float = seam_map.astype(jnp.float32)
    w_down = (0.5 + 0.5 * seam_float[position]).astype(jnp.bfloat16)
    w_up = (0.5 + 0.5 * seam_float[(position + strips - 1) % strips]).astype(jnp.bfloat16)

    own = coeffs.transpose(1, 0, 2)
    low, high = rims(own)
    coef_cols = columns(jnp.concatenate([low * w_up, own, high * w_down], axis=0), width)
    taps = dictionary.reshape(local_atoms, chans, TAP, TAP).transpose(2, 3, 0, 1)
    partial_value = apply_band(coef_cols, banded(taps), strip_rows)
    share = lax.psum_scatter(partial_value, "atom", scatter_dimension=1, tiled=True)
    band_count = share.shape[1]
    own_bands = lax.dynamic_slice_in_dim(image, lax.axis_index("atom") * band_count, band_count, 0)
    resid_share = (own_bands.transpose(1, 0, 2).astype(jnp.float32) - share).astype(jnp.bfloat16)
    low, high = rims(resid_share)
    share_padded = jnp.concatenate([low * w_up, resid_share, high * w_down], axis=0)
    resid_padded = lax.all_gather(share_padded, "atom", axis=1, tiled=True)
    residual = resid_padded[RIM : RIM + strip_rows].transpose(1, 0, 2)
    resid_cols = columns(resid_padded, width)
    flipped = taps[::-1, ::-1].transpose(0, 1, 3, 2)

    terms = 0.0
    for start, window in windows(resid_cols, strip_rows):
        rows = own[start : start + BLOCK].reshape(BLOCK * local_atoms, width)
        terms += lax.dot_general(
            window, rows, (((1,), (1,)), ((), ())), preferred_element_type=jnp.float32
        )
    terms = terms.reshape(SPAN, TAP, chans, BLOCK * local_atoms)
    summed = sum(
        terms[j : j + TAP, :, :, j * local_atoms : (j + 1) * local_atoms] for j in range(BLOCK)
    )
    scale = 1.0 / jnp.sqrt(jnp.float32(strip_rows * strips * width))
    part = lax.psum_scatter(summed * scale, "tile", scatter_dimension=2, tiled=True)
    atom_step = part[::-1, ::-1].transpose(3, 2, 0, 1).reshape(local_atoms, -1)

    correlation = apply_band(resid_cols, banded(flipped), strip_rows).transpose(1, 0, 2)
    updated = coeffs.astype(jnp.float32) + step_size * correlation
    new_coeffs = (
        updated - shrink[:, None, None] * updated / jnp.sqrt(updated * updated + eps_sq)
    ).astype(jnp.bfloat16)
    return (new_coeffs, residual, atom_step)


def solution(mesh):
    placed = (P(None, "tile", None), P("atom", "tile", None), P("atom", None), P("atom"), P())
    return jax.shard_map(
        per_device,
        mesh=mesh,
        in_specs=placed,
        out_specs=(P("atom", "tile", None), P(None, "tile", None), P("atom", "tile")),
        check_vma=False,
    )
```

```python
import jax
import jax.numpy as jnp
from jax import lax
from jax.experimental import pallas as pl
from jax.experimental.pallas import tpu as pltpu
from jax.sharding import PartitionSpec as P

TAP = 9
RIM = TAP // 2
BLOCK = 4
SPAN = BLOCK + TAP - 1

step_size = 0.1
eps_sq = 0.01


def greet(axis, count, me):
    barrier = pltpu.get_barrier_semaphore()
    for step in range(1, count):
        pl.semaphore_signal(
            barrier,
            inc=1,
            device_id={axis: lax.rem(me + step, count)},
            device_id_type=pl.DeviceIdType.MESH,
        )
    pl.semaphore_wait(barrier, count - 1)


def scatter_sum(blocks, axis, call_id):
    count = blocks.shape[0]
    piece = blocks.shape[1:]

    def kernel(x_ref, o_ref, held, send_sem, recv_sem):
        me = lax.axis_index(axis)
        greet(axis, count, me)
        copies = []
        for step in range(1, count):
            peer = lax.rem(me + step, count)
            copy = pltpu.make_async_remote_copy(
                src_ref=x_ref.at[peer],
                dst_ref=held.at[step - 1],
                send_sem=send_sem.at[step - 1],
                recv_sem=recv_sem.at[step - 1],
                device_id={axis: peer},
                device_id_type=pl.DeviceIdType.MESH,
            )
            copy.start()
            copies.append(copy)
        for copy in copies:
            copy.wait()
        total = x_ref[me].astype(jnp.float32)
        for step in range(1, count):
            total += held[step - 1].astype(jnp.float32)
        o_ref[...] = total

    return pl.pallas_call(
        kernel,
        out_shape=jax.ShapeDtypeStruct(piece, jnp.float32),
        in_specs=[pl.BlockSpec(memory_space=pltpu.VMEM)],
        out_specs=pl.BlockSpec(memory_space=pltpu.VMEM),
        scratch_shapes=[
            pltpu.VMEM((count - 1,) + piece, blocks.dtype),
            pltpu.SemaphoreType.DMA((count - 1,)),
            pltpu.SemaphoreType.DMA((count - 1,)),
        ],
        compiler_params=pltpu.CompilerParams(collective_id=call_id, has_side_effects=True),
    )(blocks)


def gather(block, axis, call_id):
    count = lax.axis_size(axis)

    def kernel(x_ref, o_ref, held, send_sem, recv_sem):
        me = lax.axis_index(axis)
        greet(axis, count, me)
        copies = []
        for step in range(1, count):
            copy = pltpu.make_async_remote_copy(
                src_ref=x_ref,
                dst_ref=held.at[step - 1],
                send_sem=send_sem.at[step - 1],
                recv_sem=recv_sem.at[step - 1],
                device_id={axis: lax.rem(me + step, count)},
                device_id_type=pl.DeviceIdType.MESH,
            )
            copy.start()
            copies.append(copy)
        o_ref[me] = x_ref[...]
        for step, copy in enumerate(copies, 1):
            copy.wait()
            o_ref[lax.rem(me + count - step, count)] = held[step - 1]

    return pl.pallas_call(
        kernel,
        out_shape=jax.ShapeDtypeStruct((count,) + block.shape, block.dtype),
        in_specs=[pl.BlockSpec(memory_space=pltpu.VMEM)],
        out_specs=pl.BlockSpec(memory_space=pltpu.VMEM),
        scratch_shapes=[
            pltpu.VMEM((count - 1,) + block.shape, block.dtype),
            pltpu.SemaphoreType.DMA((count - 1,)),
            pltpu.SemaphoreType.DMA((count - 1,)),
        ],
        compiler_params=pltpu.CompilerParams(collective_id=call_id, has_side_effects=True),
    )(block)


def rims(block):
    count = lax.axis_size("tile")
    forward = [(i, (i + 1) % count) for i in range(count)]
    backward = [(target, source) for source, target in forward]
    low = lax.ppermute(block[-RIM:], "tile", forward)
    high = lax.ppermute(block[:RIM], "tile", backward)
    return low, high


def columns(padded, width):
    wide = jnp.pad(padded, ((0, 0), (0, 0), (RIM, RIM)))
    return jnp.stack([wide[:, :, d : d + width] for d in range(TAP)], axis=1)


def banded(taps):
    parts = [
        jnp.pad(taps, ((j, BLOCK - 1 - j), (0, 0), (0, 0), (0, 0))) for j in range(BLOCK)
    ]
    return jnp.concatenate(parts, axis=3).reshape(SPAN * TAP * taps.shape[2], -1)


def windows(cols, rows):
    for start in range(0, rows, BLOCK):
        part = cols[start : start + SPAN]
        yield start, part.reshape(-1, part.shape[-1])


def apply_band(cols, band, rows):
    outs = []
    for _, window in windows(cols, rows):
        outs.append(
            lax.dot_general(
                band, window, (((0,), (0,)), ((), ())), preferred_element_type=jnp.float32
            )
        )
    return jnp.concatenate(outs, axis=0).reshape(rows, -1, cols.shape[-1])


def per_device(image, coeffs, dictionary, shrink, seam_map):
    local_atoms, strip_rows, width = coeffs.shape
    chans = image.shape[0]
    strips = lax.axis_size("tile")
    position = lax.axis_index("tile")
    seam_float = seam_map.astype(jnp.float32)
    w_down = (0.5 + 0.5 * seam_float[position]).astype(jnp.bfloat16)
    w_up = (0.5 + 0.5 * seam_float[(position + strips - 1) % strips]).astype(jnp.bfloat16)

    own = coeffs.transpose(1, 0, 2)
    low, high = rims(own)
    coef_cols = columns(jnp.concatenate([low * w_up, own, high * w_down], axis=0), width)
    taps = dictionary.reshape(local_atoms, chans, TAP, TAP).transpose(2, 3, 0, 1)
    partial_value = apply_band(coef_cols, banded(taps), strip_rows)
    groups = lax.axis_size("atom")
    band_count = chans // groups
    pieces = partial_value.reshape(strip_rows, groups, band_count, width).transpose(1, 0, 2, 3)
    share = scatter_sum(pieces.reshape(groups, -1, width), "atom", 0)
    share = share.reshape(strip_rows, band_count, width)
    own_bands = lax.dynamic_slice_in_dim(image, lax.axis_index("atom") * band_count, band_count, 0)
    resid_share = (own_bands.transpose(1, 0, 2).astype(jnp.float32) - share).astype(jnp.bfloat16)
    low, high = rims(resid_share)
    share_padded = jnp.concatenate([low * w_up, resid_share, high * w_down], axis=0)
    padded_rows = share_padded.shape[0]
    resid_all = gather(share_padded.reshape(-1, width), "atom", 1)
    resid_all = resid_all.reshape(groups, padded_rows, band_count, width)
    resid_padded = resid_all.transpose(1, 0, 2, 3).reshape(padded_rows, chans, width)
    residual = resid_padded[RIM : RIM + strip_rows].transpose(1, 0, 2)
    resid_cols = columns(resid_padded, width)
    flipped = taps[::-1, ::-1].transpose(0, 1, 3, 2)

    terms = 0.0
    for start, window in windows(resid_cols, strip_rows):
        rows = own[start : start + BLOCK].reshape(BLOCK * local_atoms, width)
        terms += lax.dot_general(
            window, rows, (((1,), (1,)), ((), ())), preferred_element_type=jnp.float32
        )
    terms = terms.reshape(SPAN, TAP, chans, BLOCK * local_atoms)
    summed = sum(
        terms[j : j + TAP, :, :, j * local_atoms : (j + 1) * local_atoms] for j in range(BLOCK)
    )
    scale = 1.0 / jnp.sqrt(jnp.float32(strip_rows * strips * width))
    half = chans // strips // 2
    sides = (summed * scale).astype(jnp.bfloat16).reshape(-1, strips, 2, half, local_atoms)
    packed = jnp.concatenate([sides[:, :, 0], sides[:, :, 1]], axis=-1).transpose(1, 0, 2, 3)
    part = scatter_sum(packed.reshape(strips, -1, 2 * local_atoms), "tile", 2)
    part = part.reshape(TAP, TAP, half, 2, local_atoms)[::-1, ::-1]
    atom_step = part.transpose(4, 3, 2, 0, 1).reshape(local_atoms, -1)

    correlation = apply_band(resid_cols, banded(flipped), strip_rows).transpose(1, 0, 2)
    updated = coeffs.astype(jnp.float32) + step_size * correlation
    new_coeffs = (
        updated - shrink[:, None, None] * updated / jnp.sqrt(updated * updated + eps_sq)
    ).astype(jnp.bfloat16)
    return (new_coeffs, residual, atom_step)


def solution(mesh):
    placed = (P(None, "tile", None), P("atom", "tile", None), P("atom", None), P("atom"), P())
    return jax.shard_map(
        per_device,
        mesh=mesh,
        in_specs=placed,
        out_specs=(P("atom", "tile", None), P(None, "tile", None), P("atom", "tile")),
        check_vma=False,
    )
```
